32 devices in a mesh: ctx: 8 (over z, x), head: 4 (over y, core).
Axes of the slice: x: 2, y: 2, z: 4, core: 2. Of those that a mesh axis runs over, the one named last changes fastest.
Arguments:
- queries: bfloat16 [6144, 4096], P('ctx', 'head'), may hold values from -20 to 20
- keys: bfloat16 [6144, 4096], P('ctx', 'head'), may hold values from -6 to 6
- values: bfloat16 [6144, 4096], P('ctx', 'head'), may hold values from -64 to 64
- cotangent: bfloat16 [6144, 4096], P('ctx', 'head'), may hold values from -6 to 6
- state_in: float32 [32, 128, 128], P('head'), may hold values from -96 to 96
Outputs:
- output: bfloat16 [6144, 4096], P('ctx', 'head')
- grad_queries: bfloat16 [6144, 4096], P('ctx', 'head')
- grad_keys: bfloat16 [6144, 4096], P('ctx', 'head')
- grad_values: bfloat16 [6144, 4096], P('ctx', 'head')
The draws below stay inside these ranges and needn't reach their ends.
All inputs are finite; a program needn't handle non-finite values.
Results may differ from the reference program's by a relative error of at most 0.0058.
Values sent between devices are 32-bit elements; how exact they have to be, the bound alone decides.
No kernel may reach another device: no remote copies, remote signals or barrier semaphores. Data moves between devices by JAX's collectives and lax.ppermute only.
A program may use at most 128 MiB of HBM per device.

```python
import math
import jax
import jax.numpy as jnp
from jax import lax

HEADS = 32
DH = 128
TOK_DEV = 768
SEQ = 6144


def draw_queries(key, part):
    entry_key, row_key = jax.random.split(jax.random.fold_in(key, 11), 2)
    feat_width = HEADS * DH
    row_scale = jnp.exp(jax.random.uniform(row_key, (SEQ, 1), jnp.float32, math.log(0.3), math.log(3.0)))
    entries = jax.random.normal(entry_key, (SEQ, feat_width), jnp.float32)
    return jnp.clip(entries * row_scale, -20.0, 20.0).astype(jnp.bfloat16)


def draw_values(key, part):
    entry_key, column_key = jax.random.split(jax.random.fold_in(key, 23), 2)
    feat_width = HEADS * DH
    head_number = (jnp.arange(feat_width) // DH).astype(jnp.float32)
    column_scale = 3.0 ** (head_number / (HEADS - 1)) * jnp.exp(jax.random.uniform(column_key, (feat_width,), jnp.float32, 0.0, math.log(3.5)))
    entries = jax.random.normal(entry_key, (SEQ, feat_width), jnp.float32)
    return jnp.clip(entries * column_scale[None, :], -64.0, 64.0).astype(jnp.bfloat16)


def block_levels(key, shape, pieces, least, largest):
    factor_of = 1.0
    for dim, parts in pieces:
        draws = jax.random.uniform(jax.random.fold_in(jax.random.fold_in(key, 6), dim), (parts,), jnp.float32, least / len(pieces), largest / len(pieces))
        factor_of = factor_of * jnp.repeat(jnp.exp(draws), shape[dim] // parts).reshape((-1,) + (1,) * (len(shape) - 1 - dim))
    return factor_of


def gaussian(rng, dims, spread, most, cuts=(), held_as=jnp.bfloat16):
    result = jax.random.normal(rng, dims, jnp.float32) * spread
    if len(cuts) > 0:
        result = block_levels(rng, dims, cuts, -0.22, 0.18) * result
    return jnp.clip(result, min=-most, max=most).astype(held_as)


def setup_inputs(seed: int = 0) -> dict:
    key_list = jax.random.split(jax.random.key(seed), 6)
    queries = draw_queries(jax.random.fold_in(key_list[5], 71), 0)
    keys = gaussian(key_list[1], (SEQ, HEADS * DH), 1.0, 6.0, ((0, 8), (1, 4)))
    values = draw_values(jax.random.fold_in(key_list[5], 71), 0)
    cotangent = gaussian(key_list[3], (SEQ, HEADS * DH), 1.0, 6.0, ((0, 8), (1, 4)))
    state_in = gaussian(key_list[4], (HEADS, DH, DH), 16.0, 96.0, ((0, 4),), jnp.float32)
    return dict(queries=queries, keys=keys, values=values, cotangent=cotangent, state_in=state_in)


def masked_product(left, right, causal_mask):
    scores = jnp.einsum('thi,shi->hts', left.astype(jnp.float32), right.astype(jnp.float32))
    return jnp.where(causal_mask[None], scores, 0.0).astype(jnp.bfloat16)

def reference(queries, keys, values, cotangent, state_in):
    seq_len = queries.shape[0]
    blocks = seq_len // TOK_DEV
    feat_count = HEADS * DH

    def split_blocks(array):
        return array.reshape(blocks, TOK_DEV, HEADS, DH)
    positions = jnp.arange(TOK_DEV)
    causal_mask = positions[:, None] >= positions[None, :]

    def forward_block(state_now, inputs):
        query_heads, key_heads, value_heads = inputs
        state_low = state_now.astype(jnp.bfloat16)
        scores = masked_product(query_heads, key_heads, causal_mask)
        attention = jnp.einsum('hts,she->the', scores.astype(jnp.float32), value_heads.astype(jnp.float32))
        attention = attention + jnp.einsum('thi,hie->the', query_heads.astype(jnp.float32), state_low.astype(jnp.float32))
        kv_block = jnp.einsum('shi,she->hie', key_heads.astype(jnp.float32), value_heads.astype(jnp.float32))
        return (state_now + kv_block, (attention, state_low))
    _, (attention, state_list) = lax.scan(forward_block, state_in, (split_blocks(queries), split_blocks(keys), split_blocks(values)))
    attention = attention.reshape(seq_len, feat_count)
    grad_float = cotangent.astype(jnp.float32)
    inverse_rms = lax.rsqrt(lax.optimization_barrier(jnp.sum(attention * attention, axis=1)) / feat_count + 1e-06)
    cross_sum = lax.optimization_barrier(jnp.sum(grad_float * attention, axis=1))
    output = (attention * inverse_rms[:, None]).astype(jnp.bfloat16)
    grad_attention = (inverse_rms[:, None] * grad_float - attention * (inverse_rms ** 3 * cross_sum / feat_count)[:, None]).astype(jnp.bfloat16)

    def backward_block(suffix_now, inputs):
        query_heads, key_heads, value_heads, grad_heads, state_low = inputs
        suffix_low = suffix_now.astype(jnp.bfloat16)
        query_float = query_heads.astype(jnp.float32)
        key_float = key_heads.astype(jnp.float32)
        value_float = value_heads.astype(jnp.float32)
        grad_f = grad_heads.astype(jnp.float32)
        scores = masked_product(query_heads, key_heads, causal_mask).astype(jnp.float32)
        grad_scores = masked_product(grad_heads, value_heads, causal_mask).astype(jnp.float32)
        grad_query = jnp.einsum('hts,shi->thi', grad_scores, key_float) + jnp.einsum('the,hie->thi', grad_f, state_low.astype(jnp.float32))
        grad_key = jnp.einsum('hts,thi->shi', grad_scores, query_float) + jnp.einsum('she,hie->shi', value_float, suffix_low.astype(jnp.float32))
        grad_value = jnp.einsum('hts,the->she', scores, grad_f) + jnp.einsum('shi,hie->she', key_float, suffix_low.astype(jnp.float32))
        qd_block = jnp.einsum('thi,the->hie', query_float, grad_f)
        return (suffix_now + qd_block, (grad_query.astype(jnp.bfloat16), grad_key.astype(jnp.bfloat16), grad_value.astype(jnp.bfloat16)))
    zero_state = jnp.zeros((HEADS, DH, DH), jnp.float32)
    _, (grad_query, grad_key, grad_value) = lax.scan(backward_block, zero_state, (split_blocks(queries), split_blocks(keys), split_blocks(values), split_blocks(grad_attention), state_list), reverse=True)
    return (output, grad_query.reshape(seq_len, feat_count), grad_key.reshape(seq_len, feat_count), grad_value.reshape(seq_len, feat_count))
```

```python
import functools

import jax
import jax.numpy as jnp
from jax import lax
from jax.experimental import pallas as pl
from jax.experimental.pallas import tpu as pltpu
from jax.sharding import PartitionSpec as P

DH = 128
QUAD = 4
ROWS = 256
F32 = jnp.float32
BF16 = jnp.bfloat16
VMEM = pltpu.VMEM
MIB = 1 << 20


def dot(a, b, da, db):
    return lax.dot_general(a, b, (((da,), (db,)), ((), ())), preferred_element_type=F32)


def resident(x):
    return pltpu.with_memory_space_constraint(x, VMEM)


def call(body, outs, args, name, flops=0, nbytes=0, scratch=(), aliases=None, limit=16):
    in_specs = [pl.BlockSpec(memory_space=VMEM if kind == "vmem" else pl.ANY) for kind, _ in args]
    out_specs = tuple(pl.BlockSpec(memory_space=VMEM if kind == "vmem" else pl.ANY) for kind, _, _ in outs)
    out_shape = tuple(
        VMEM(shape, dtype) if kind == "vmem" else jax.ShapeDtypeStruct(shape, dtype) for kind, shape, dtype in outs
    )
    operands = [resident(x) if kind == "vmem" else x for kind, x in args]
    return pl.pallas_call(
        body,
        out_shape=out_shape,
        in_specs=in_specs,
        out_specs=out_specs,
        scratch_shapes=list(scratch),
        input_output_aliases=aliases or {},
        name=name,
        cost_estimate=pl.CostEstimate(flops=flops, transcendentals=0, bytes_accessed=nbytes),
        compiler_params=pltpu.CompilerParams(vmem_limit_bytes=limit * MIB),
    )(*operands)


def place():
    return lax.axis_index("ctx") % QUAD


def columns(slot, head, heads_own):
    owner = place() ^ slot if slot else place()
    return pl.multiple_of((owner * heads_own + head) * DH, DH)


def wide(slot, heads_own):
    owner = place() ^ slot if slot else place()
    return pl.multiple_of(owner * (heads_own * DH), DH)


def xor_permute(x, axis, k):
    return lax.ppermute(x, axis, [(i, i ^ k) for i in range(lax.axis_size(axis))])


def outer_remote_body(heads_own, k_hbm, v_hbm, *refs):
    outs, (kb, vb, sems) = refs[: QUAD - 1], refs[QUAD - 1 :]
    width = heads_own * DH
    copies = []
    for slot in range(1, QUAD):
        at = pl.ds(wide(slot, heads_own), width)
        ck = pltpu.make_async_copy(k_hbm.at[:, at], kb.at[slot - 1], sems.at[0, slot - 1])
        cv = pltpu.make_async_copy(v_hbm.at[:, at], vb.at[slot - 1], sems.at[1, slot - 1])
        ck.start()
        cv.start()
        copies.append((ck, cv))
    for slot in range(1, QUAD):
        for c in copies[slot - 1]:
            c.wait()
        for h in range(heads_own):
            at = slice(h * DH, (h + 1) * DH)
            outs[slot - 1][h] = dot(kb[slot - 1, :, at], vb[slot - 1, :, at], 0, 0)


def outer_own_body(heads_own, k, v, out):
    for h in range(heads_own):
        at = pl.ds(columns(0, h, heads_own), DH)
        out[h] = dot(k[:, at], v[:, at], 0, 0)


def masked(scores, first_row, first_col, transposed):
    rows = lax.broadcasted_iota(jnp.int32, scores.shape, 0) + first_row
    cols = lax.broadcasted_iota(jnp.int32, scores.shape, 1) + first_col
    keep = rows <= cols if transposed else rows >= cols
    return jnp.where(keep, scores, 0.0).astype(BF16)


def local_attention_body(slots, heads_own, q, k, v, *outs):
    blocks = q.shape[0] // ROWS
    for out, slot in zip(outs, slots):
        for h in range(heads_own):
            at = pl.ds(columns(slot, h, heads_own), DH)
            to = slice(h * DH, (h + 1) * DH)
            for i in range(blocks):
                lo, hi = i * ROWS, (i + 1) * ROWS
                qi = q[lo:hi, at]
                diag = masked(dot(qi, k[lo:hi, at], 1, 1), 0, 0, False)
                acc = dot(diag, v[lo:hi, at], 1, 0)
                if i:
                    low = dot(qi, k[0:lo, at], 1, 1).astype(BF16)
                    acc = acc + dot(low, v[0:lo, at], 1, 0)
                out[lo:hi, to] = acc


def total_body(*refs):
    out = refs[-1]
    total = refs[0][...]
    for r in refs[1:-1]:
        total = total + r[...]
    out[...] = total


def spread_body(heads_own, forward, with_state, rounds, *refs):
    received, refs = refs[:QUAD], refs[QUAD:]
    others, refs = refs[:rounds], refs[rounds:]
    if with_state:
        state, refs = refs[0], refs[1:]
    outs = refs
    me = place()
    base = None
    if with_state:
        base = state[pl.ds(me * heads_own, heads_own)]
    group = lax.axis_index("ctx") // QUAD
    for d, r in enumerate(others):
        bit = (group >> d) & 1
        keep = bit == (1 if forward else 0)
        term = jnp.where(keep, r[...], 0.0)
        base = term if base is None else base + term
    for j in range(QUAD):
        target = me ^ j
        total = base
        for i in range(QUAD):
            if i == j:
                continue
            source = me ^ i
            keep = source < target if forward else source > target
            term = jnp.where(keep, received[i][...], 0.0)
            total = term if total is None else total + term
        outs[j][...] = total


def attend(slot, heads_own, q, g, local, state, att, low, sq, cr):
    for h in range(heads_own):
        at = pl.ds(columns(slot, h, heads_own), DH)
        to = slice(h * DH, (h + 1) * DH)
        state_low = state[h].astype(BF16)
        low[h] = state_low
        a = local[:, to] + dot(q[:, at], state_low, 1, 0)
        att[:, to] = a
        sq = sq + a * a
        cr = cr + a * g[:, at].astype(F32)
    return sq, cr


def attend_own_body(heads_own, q, g, local, state, att, low, sq_out, cr_out):
    zero = jnp.zeros((q.shape[0], DH), F32)
    sq, cr = attend(0, heads_own, q, g, local, state, att, low, zero, zero)
    sq_out[...] = sq
    cr_out[...] = cr


def attend_remote_body(heads_own, q, g, sq_in, cr_in, *refs):
    n = QUAD - 1
    locals_, states = refs[:n], refs[n : 2 * n]
    atts, lows, stats = refs[2 * n : 3 * n], refs[3 * n : 4 * n], refs[4 * n]
    sq, cr = sq_in[...], cr_in[...]
    for s in range(n):
        sq, cr = attend(s + 1, heads_own, q, g, locals_[s], states[s], atts[s], lows[s], sq, cr)
    stats[0:1, :] = jnp.sum(sq.T, axis=0, keepdims=True)
    stats[1:2, :] = jnp.sum(cr.T, axis=0, keepdims=True)


def backprop_norm(slot, heads_own, q, g, att, inv, coef, d_out, qd_out):
    for h in range(heads_own):
        at = pl.ds(columns(slot, h, heads_own), DH)
        to = slice(h * DH, (h + 1) * DH)
        d = (inv * g[:, at].astype(F32) - att[:, to] * coef).astype(BF16)
        d_out[:, to] = d
        qd_out[h] = dot(q[:, at], d, 0, 0)


def norm_remote_body(heads_own, feat_count, parts, q, g, *refs):
    n = QUAD - 1
    stats, refs = refs[:parts], refs[parts:]
    atts, refs = refs[:n], refs[n:]
    ds, qds, inv_out, coef_out = refs[:n], refs[n : 2 * n], refs[2 * n], refs[2 * n + 1]
    both = stats[0][...]
    for s in stats[1:]:
        both = both + s[...]
    inv = lax.rsqrt(both[0:1, :] / feat_count + 1e-06)
    coef = inv * inv * inv * both[1:2, :] / feat_count
    tok = q.shape[0]
    inv_out[...] = jnp.broadcast_to(inv, (DH, tok)).T
    coef_out[...] = jnp.broadcast_to(coef, (DH, tok)).T
    inv, coef = inv_out[...], coef_out[...]
    for s in range(n):
        backprop_norm(s + 1, heads_own, q, g, atts[s], inv, coef, ds[s], qds[s])


def norm_own_body(heads_own, q, g, att, inv, coef, d_out, qd_out):
    backprop_norm(0, heads_own, q, g, att, inv[...], coef[...], d_out, qd_out)


def output_body(heads_own, inv, *refs):
    atts, out, buf, sems = refs[:QUAD], refs[QUAD], refs[QUAD + 1], refs[QUAD + 2]
    width = heads_own * DH
    scale = inv[...]
    copies = []
    for slot in range(QUAD):
        for h in range(heads_own):
            to = slice(h * DH, (h + 1) * DH)
            buf[slot, :, to] = (atts[slot][:, to] * scale).astype(BF16)
        c = pltpu.make_async_copy(buf.at[slot], out.at[:, pl.ds(wide(slot, heads_own), width)], sems.at[slot])
        c.start()
        copies.append(c)
    for c in copies:
        c.wait()


def local_grads_body(slot, heads_own, q, k, v, d, low, *refs):
    gq_hbm, gk, gv, buf, sem = refs[-5:]
    blocks = q.shape[0] // ROWS
    tok = q.shape[0]
    for h in range(heads_own):
        at = pl.ds(columns(slot, h, heads_own), DH)
        to = slice(h * DH, (h + 1) * DH)
        for i in range(blocks):
            lo, hi = i * ROWS, (i + 1) * ROWS
            di = d[lo:hi, to]
            acc = dot(di, low[h], 1, 1)
            diag = masked(dot(di, v[lo:hi, at], 1, 1), 0, 0, False)
            acc = acc + dot(diag, k[lo:hi, at], 1, 0)
            if i:
                rest = dot(di, v[0:lo, at], 1, 1).astype(BF16)
                acc = acc + dot(rest, k[0:lo, at], 1, 0)
            buf[lo:hi, to] = acc.astype(BF16)
            ki, vi = k[lo:hi, at], v[lo:hi, at]
            diag = masked(dot(ki, q[lo:hi, at], 1, 1), 0, 0, True)
            acc_v = dot(diag, di, 1, 0)
            diag = masked(dot(vi, di, 1, 1), 0, 0, True)
            acc_k = dot(diag, q[lo:hi, at], 1, 0)
            if hi < tok:
                rest = dot(ki, q[hi:tok, at], 1, 1).astype(BF16)
                acc_v = acc_v + dot(rest, d[hi:tok, to], 1, 0)
                rest = dot(vi, d[hi:tok, to], 1, 1).astype(BF16)
                acc_k = acc_k + dot(rest, q[hi:tok, at], 1, 0)
            gv[lo:hi, to] = acc_v
            gk[lo:hi, to] = acc_k
    width = heads_own * DH
    c = pltpu.make_async_copy(buf, gq_hbm.at[:, pl.ds(wide(slot, heads_own), width)], sem)
    c.start()
    c.wait()


def final_body(slots, heads_own, k, v, *refs):
    n = len(slots)
    gks, gvs, sufs, refs = refs[:n], refs[n : 2 * n], refs[2 * n : 3 * n], refs[3 * n :]
    gk_hbm, gv_hbm, kbuf, vbuf, sems = refs[-5:]
    width = heads_own * DH
    copies = []
    for s, slot in enumerate(slots):
        for h in range(heads_own):
            at = pl.ds(columns(slot, h, heads_own), DH)
            to = slice(h * DH, (h + 1) * DH)
            suffix = sufs[s][h].astype(BF16)
            kbuf[s, :, to] = (gks[s][:, to] + dot(v[:, at], suffix, 1, 1)).astype(BF16)
            vbuf[s, :, to] = (gvs[s][:, to] + dot(k[:, at], suffix, 1, 0)).astype(BF16)
        cols = pl.ds(wide(slot, heads_own), width)
        for which, (buf, hbm) in enumerate(((kbuf, gk_hbm), (vbuf, gv_hbm))):
            c = pltpu.make_async_copy(buf.at[s], hbm.at[:, cols], sems.at[which, s])
            c.start()
            copies.append(c)
    for c in copies:
        c.wait()


def scan_quads(parts_remote, own, heads_own, forward, state, name):
    shape = own.shape
    n_groups = lax.axis_size("ctx") // QUAD
    received = [own] + [xor_permute(parts_remote[j - 1], "ctx", j) for j in range(1, QUAD)]
    total = call(total_body, [("vmem", shape, F32)], [("vmem", r) for r in received], name + "_total", nbytes=1 << 19)[0]
    others = []
    d = 1
    while d < n_groups:
        other = xor_permute(total, "ctx", QUAD * d)
        others.append(other)
        d *= 2
        if d < n_groups:
            total = call(
                total_body, [("vmem", shape, F32)], [("vmem", total), ("vmem", other)], name + "_more", nbytes=1 << 19
            )[0]
    args = [("vmem", r) for r in received + others]
    if state is not None:
        args.append(("vmem", state))
    outs = call(
        functools.partial(spread_body, heads_own, forward, state is not None, len(others)),
        [("vmem", shape, F32)] * QUAD,
        args,
        name + "_spread",
        nbytes=1 << 20,
    )
    return [outs[0]] + [xor_permute(outs[j], "ctx", j) for j in range(1, QUAD)]


def local(queries, keys, values, cotangent, state_in):
    tok, feat_here = queries.shape
    heads_here = feat_here // DH
    heads_own = heads_here // QUAD
    width = heads_own * DH
    n_head = lax.axis_size("head")
    feat_count = feat_here * n_head
    part = (heads_own, DH, DH)
    q, k, v, g = (("vmem", x) for x in (queries, keys, values, cotangent))
    remote = range(1, QUAD)
    state_flops = 2 * tok * DH * DH * heads_own
    score_flops = 4 * tok * tok * DH * heads_own

    kv_remote = call(
        functools.partial(outer_remote_body, heads_own),
        [("vmem", part, F32)] * (QUAD - 1),
        [("hbm", keys), ("hbm", values)],
        "kv_remote",
        flops=3 * state_flops,
        nbytes=3 * MIB,
        scratch=[
            VMEM((QUAD - 1, tok, width), BF16),
            VMEM((QUAD - 1, tok, width), BF16),
            pltpu.SemaphoreType.DMA((2, QUAD - 1)),
        ],
    )
    kv_own = call(
        functools.partial(outer_own_body, heads_own), [("vmem", part, F32)], [k, v], "kv_own", flops=state_flops
    )[0]
    locals_ = []
    for slots in ((0,), (1,), (2,), (3,)):
        locals_ += call(
            functools.partial(local_attention_body, slots, heads_own),
            [("vmem", (tok, width), F32)] * len(slots),
            [q, k, v],
            "local_attention",
            flops=score_flops * len(slots),
        )
    states = scan_quads(kv_remote, kv_own, heads_own, True, state_in, "prefix")

    wide_f32 = ("vmem", (tok, width), F32)
    wide_low = ("vmem", (tok, width), BF16)
    state_low = ("vmem", part, BF16)
    rows = ("vmem", (tok, DH), F32)
    att_own, low_own, sq, cr = call(
        functools.partial(attend_own_body, heads_own),
        [wide_f32, state_low, rows, rows],
        [q, g, ("vmem", locals_[0]), ("vmem", states[0])],
        "attend_own",
        flops=state_flops,
    )
    outs = call(
        functools.partial(attend_remote_body, heads_own),
        [wide_f32] * 3 + [state_low] * 3 + [("vmem", (2, tok), F32)],
        [q, g, ("vmem", sq), ("vmem", cr)] + [("vmem", x) for x in locals_[1:] + states[1:]],
        "attend_remote",
        flops=3 * state_flops,
    )
    atts, lows, stats = [att_own, *outs[:3]], [low_own, *outs[3:6]], outs[6]
    all_stats = [stats] + [xor_permute(stats, "head", i) for i in range(1, n_head)]
    outs = call(
        functools.partial(norm_remote_body, heads_own, feat_count, n_head),
        [wide_low] * 3 + [("vmem", part, F32)] * 3 + [rows, rows],
        [q, g] + [("vmem", x) for x in all_stats + atts[1:]],
        "norm_remote",
        flops=3 * state_flops,
    )
    d_remote, qd_remote, inv, coef = outs[:3], outs[3:6], outs[6], outs[7]
    d_own, qd_own = call(
        functools.partial(norm_own_body, heads_own),
        [wide_low, ("vmem", part, F32)],
        [q, g, ("vmem", att_own), ("vmem", inv), ("vmem", coef)],
        "norm_own",
        flops=state_flops,
    )
    ds = [d_own, *d_remote]
    output = call(
        functools.partial(output_body, heads_own),
        [("hbm", (tok, feat_here), BF16)],
        [("vmem", inv)] + [("vmem", a) for a in atts],
        "output",
        nbytes=3 * MIB // 2,
        scratch=[VMEM((QUAD, tok, width), BF16), pltpu.SemaphoreType.DMA((QUAD,))],
    )[0]
    gks, gvs = [], []
    grad_query = None
    for slot in range(QUAD):
        args = [q, k, v, ("vmem", ds[slot]), ("vmem", lows[slot])]
        aliases = {}
        if grad_query is not None:
            aliases = {len(args): 0}
            args.append(("hbm", grad_query))
        grad_query, gk, gv = call(
            functools.partial(local_grads_body, slot, heads_own),
            [("hbm", (tok, feat_here), BF16), wide_f32, wide_f32],
            args,
            "local_grads",
            flops=3 * score_flops,
            scratch=[VMEM((tok, width), BF16), pltpu.SemaphoreType.DMA],
            aliases=aliases,
        )
        gks.append(gk)
        gvs.append(gv)
    suffixes = scan_quads(qd_remote, qd_own, heads_own, False, None, "suffix")
    full = ("hbm", (tok, feat_here), BF16)
    grads = ()
    for slots in ((0,), tuple(remote)):
        args = [k, v] + [("vmem", x[s]) for x in (gks, gvs, suffixes) for s in slots]
        aliases = {len(args) + i: i for i in range(len(grads))}
        args += [("hbm", x) for x in grads]
        grads = call(
            functools.partial(final_body, slots, heads_own),
            [full, full],
            args,
            "final_grads",
            flops=2 * len(slots) * state_flops,
            scratch=[
                VMEM((len(slots), tok, width), BF16),
                VMEM((len(slots), tok, width), BF16),
                pltpu.SemaphoreType.DMA((2, len(slots))),
            ],
            aliases=aliases,
        )
    return output, grad_query, grads[0], grads[1]


def solution(mesh):
    wide_spec = P("ctx", "head")
    return jax.shard_map(
        local,
        mesh=mesh,
        in_specs=(wide_spec,) * 4 + (P("head", None, None),),
        out_specs=(wide_spec,) * 4,
        check_vma=False,
    )
```

```python
import functools

import jax
import jax.numpy as jnp
from jax import lax
from jax.experimental import pallas as pl
from jax.experimental.pallas import tpu as pltpu
from jax.sharding import PartitionSpec as P


DH = 128
QUAD = 4
ROWS = 256
F32 = jnp.float32
BF16 = jnp.bfloat16
VMEM = pltpu.VMEM
MIB = 1 << 20
ORDER = (1, 2, 3, 0)
FORWARD_PLACES = (0, 1, 2, 3)
BACKWARD_PLACES = (0, 1, 2, 3)
NORM_PLACES = ((1,), (2, 3), (0,))


def dot(a, b, da, db):
    return lax.dot_general(a, b, (((da,), (db,)), ((), ())), preferred_element_type=F32)


def resident(x):
    return pltpu.with_memory_space_constraint(x, VMEM)


def call(body, outs, args, flops=0, nbytes=0, scratch=(), aliases=None, limit=16):
    in_specs = [pl.BlockSpec(memory_space=VMEM if kind == "vmem" else pl.ANY) for kind, _ in args]
    out_specs = tuple(pl.BlockSpec(memory_space=VMEM if kind == "vmem" else pl.ANY) for kind, _, _ in outs)
    out_shape = tuple(
        VMEM(shape, dtype) if kind == "vmem" else jax.ShapeDtypeStruct(shape, dtype) for kind, shape, dtype in outs
    )
    operands = [resident(x) if kind == "vmem" else x for kind, x in args]
    return pl.pallas_call(
        body,
        out_shape=out_shape,
        in_specs=in_specs,
        out_specs=out_specs,
        scratch_shapes=list(scratch),
        input_output_aliases=aliases or {},
        cost_estimate=pl.CostEstimate(flops=flops, transcendentals=0, bytes_accessed=nbytes),
        compiler_params=pltpu.CompilerParams(vmem_limit_bytes=limit * MIB),
    )(*operands)


def place():
    return lax.axis_index("ctx") % QUAD


def columns(slot, head, heads_own):
    owner = place() ^ slot if slot else place()
    return pl.multiple_of((owner * heads_own + head) * DH, DH)


def wide(slot, heads_own):
    owner = place() ^ slot if slot else place()
    return pl.multiple_of(owner * (heads_own * DH), DH)


def xor_permute(x, axis, k):
    return lax.ppermute(x, axis, [(i, i ^ k) for i in range(lax.axis_size(axis))])


def outer_remote_body(heads_own, k_hbm, v_hbm, *refs):
    outs, (kr, vr, sems) = refs[: QUAD - 1], refs[QUAD - 1 :]
    width = heads_own * DH
    copies = []
    for i, slot in enumerate(ORDER):
        at = pl.ds(wide(slot, heads_own), width)
        pair = (
            pltpu.make_async_copy(k_hbm.at[:, at], kr.at[:, at], sems.at[0, i]),
            pltpu.make_async_copy(v_hbm.at[:, at], vr.at[:, at], sems.at[1, i]),
        )
        for c in pair:
            c.start()
        copies.append(pair)
    for i, slot in enumerate(ORDER):
        for c in copies[i]:
            c.wait()
        if slot:
            for h in range(heads_own):
                at = pl.ds(columns(slot, h, heads_own), DH)
                outs[slot - 1][h] = dot(kr[:, at], vr[:, at], 0, 0)


def outer_own_body(heads_own, k, v, out):
    for h in range(heads_own):
        at = pl.ds(columns(0, h, heads_own), DH)
        out[h] = dot(k[:, at], v[:, at], 0, 0)


def causal(scores):
    rows = lax.broadcasted_iota(jnp.int32, scores.shape, 0)
    cols = lax.broadcasted_iota(jnp.int32, scores.shape, 1)
    return jnp.where(rows <= cols, scores, 0.0).astype(BF16)


def row_blocks(tok):
    return [(lo, lo + ROWS) for lo in range(0, tok, ROWS)]


def local_attention_body(slot, heads_own, q, k, v, out, st, qt):
    tok = q.shape[0]

    def one(h, carry):
        at = pl.ds(columns(slot, h, heads_own), DH)
        to = pl.ds(pl.multiple_of(h * DH, DH), DH)
        for lo, hi in row_blocks(tok):
            ki = k[lo:hi, at]
            st[h, lo:hi, lo:hi] = causal(dot(ki, q[lo:hi, at], 1, 1))
            if hi < tok:
                st[h, lo:hi, hi:tok] = dot(ki, q[hi:tok, at], 1, 1).astype(BF16)
        for lo, hi in row_blocks(tok):
            out[lo:hi, to] = dot(st[h, 0:hi, lo:hi], v[0:hi, at], 0, 0)
        qt[to, :] = q[:, at].T
        return carry

    lax.fori_loop(0, heads_own, one, 0)


def total_body(*refs):
    out = refs[-1]
    total = refs[0][...]
    for r in refs[1:-1]:
        total = total + r[...]
    out[...] = total


def spread_body(heads_own, forward, with_state, rounds, *refs):
    received, refs = refs[:QUAD], refs[QUAD:]
    others, refs = refs[:rounds], refs[rounds:]
    if with_state:
        state, refs = refs[0], refs[1:]
    outs = refs
    me = place()
    base = None
    if with_state:
        base = state[pl.ds(me * heads_own, heads_own)]
    group = lax.axis_index("ctx") // QUAD
    for d, r in enumerate(others):
        bit = (group >> d) & 1
        keep = bit == (1 if forward else 0)
        term = jnp.where(keep, r[...], 0.0)
        base = term if base is None else base + term
    for j in range(QUAD):
        target = me ^ j
        total = base
        for i in range(QUAD):
            if i == j:
                continue
            source = me ^ i
            keep = source < target if forward else source > target
            term = jnp.where(keep, received[i][...], 0.0)
            total = term if total is None else total + term
        outs[j][...] = total


def attend_body(slot, heads_own, first, last, q, g, local, state, *refs):
    if not first:
        (sq_in, cr_in), refs = refs[:2], refs[2:]
    att, low, refs = refs[0], refs[1], refs[2:]
    tok = q.shape[0]
    for h in range(heads_own):
        low[h] = state[h].astype(BF16)
    for lo in range(0, tok, DH):
        hi = lo + DH
        sq = cr = None
        if not first:
            sq, cr = sq_in[lo:hi, :], cr_in[lo:hi, :]
        for h in range(heads_own):
            at = pl.ds(columns(slot, h, heads_own), DH)
            to = slice(h * DH, (h + 1) * DH)
            a = local[lo:hi, to] + dot(q[lo:hi, at], low[h], 1, 0)
            att[lo:hi, to] = a
            b = a * g[lo:hi, at].astype(F32)
            sq = a * a if sq is None else sq + a * a
            cr = b if cr is None else cr + b
        if last:
            stats = refs[0]
            stats[0:1, lo:hi] = jnp.sum(sq.T, axis=0, keepdims=True)
            stats[1:2, lo:hi] = jnp.sum(cr.T, axis=0, keepdims=True)
        else:
            refs[0][lo:hi, :] = sq
            refs[1][lo:hi, :] = cr


def norm_body(slots, heads_own, feat_count, parts, g, *refs):
    n = len(slots)
    tok = g.shape[0]
    if parts:
        stats, refs = refs[:parts], refs[parts:]
        inv_ref, coef_ref, refs = refs[-2], refs[-1], refs[:-2]
        both = stats[0][...]
        for s in stats[1:]:
            both = both + s[...]
        inv_row = lax.rsqrt(both[0:1, :] / feat_count + 1e-06)
        coef_row = inv_row * inv_row * inv_row * both[1:2, :] / feat_count
        for lo in range(0, tok, DH):
            at = slice(lo, lo + DH)
            inv_ref[at, :] = jnp.broadcast_to(inv_row[:, at], (DH, DH)).T
            coef_ref[at, :] = jnp.broadcast_to(coef_row[:, at], (DH, DH)).T
    else:
        inv_ref, coef_ref, refs = refs[0], refs[1], refs[2:]
    atts, qts, ds, qds = refs[:n], refs[n : 2 * n], refs[2 * n : 3 * n], refs[3 * n : 4 * n]
    for s, slot in enumerate(slots):
        for h in range(heads_own):
            at = pl.ds(columns(slot, h, heads_own), DH)
            to = slice(h * DH, (h + 1) * DH)
            for lo in range(0, tok, DH):
                r = slice(lo, lo + DH)
                d = inv_ref[r, :] * g[r, at].astype(F32) - atts[s][r, to] * coef_ref[r, :]
                ds[s][r, to] = d.astype(BF16)
            qds[s][h] = dot(qts[s][to, :], ds[s][:, to], 1, 0)


def output_body(heads_own, inv, *refs):
    atts, out = refs[:QUAD], refs[QUAD]
    tok = inv.shape[0]
    for lo in range(0, tok, DH):
        r = slice(lo, lo + DH)
        scale = inv[r, :]
        for slot in range(QUAD):
            for h in range(heads_own):
                a = atts[slot][r, h * DH : (h + 1) * DH]
                out[r, pl.ds(columns(slot, h, heads_own), DH)] = (a * scale).astype(BF16)


def local_grads_body(slot, heads_own, q, k, v, d, low, st, *refs):
    gq, gk, gv, dst = refs[-4:]
    tok = q.shape[0]

    def one(h, carry):
        at = pl.ds(columns(slot, h, heads_own), DH)
        to = pl.ds(pl.multiple_of(h * DH, DH), DH)
        for lo, hi in row_blocks(tok):
            vi = v[lo:hi, at]
            dst[lo:hi, lo:hi] = causal(dot(vi, d[lo:hi, to], 1, 1))
            if hi < tok:
                dst[lo:hi, hi:tok] = dot(vi, d[hi:tok, to], 1, 1).astype(BF16)
            gv[lo:hi, to] = dot(st[h, lo:hi, lo:tok], d[lo:tok, to], 1, 0)
            gk[lo:hi, to] = dot(dst[lo:hi, lo:tok], q[lo:tok, at], 1, 0)
        for lo, hi in row_blocks(tok):
            acc = dot(d[lo:hi, to], low[h], 1, 1) + dot(dst[0:hi, lo:hi], k[0:hi, at], 0, 0)
            gq[lo:hi, at] = acc.astype(BF16)
        return carry

    lax.fori_loop(0, heads_own, one, 0)


def final_body(slot, heads_own, k, v, gk, gv, suf, *refs):
    gk_hbm, gv_hbm, kbuf, vbuf, sems = refs[-5:]
    copies = []
    for h in range(heads_own):
        at = pl.ds(columns(slot, h, heads_own), DH)
        to = slice(h * DH, (h + 1) * DH)
        suffix = suf[h].astype(BF16)
        kbuf[:, to] = (gk[:, to] + dot(v[:, at], suffix, 1, 1)).astype(BF16)
        c = pltpu.make_async_copy(kbuf.at[:, to], gk_hbm.at[:, at], sems.at[0, h])
        c.start()
        copies.append(c)
        vbuf[:, to] = (gv[:, to] + dot(k[:, at], suffix, 1, 0)).astype(BF16)
        c = pltpu.make_async_copy(vbuf.at[:, to], gv_hbm.at[:, at], sems.at[1, h])
        c.start()
        copies.append(c)
    for c in copies:
        c.wait()


def scan_quads(parts_remote, own, heads_own, forward, state):
    shape = own.shape
    n_groups = lax.axis_size("ctx") // QUAD
    received = [own] + [xor_permute(parts_remote[j - 1], "ctx", j) for j in range(1, QUAD)]
    total = call(total_body, [("vmem", shape, F32)], [("vmem", r) for r in received], nbytes=1 << 19)[0]
    others = []
    d = 1
    while d < n_groups:
        other = xor_permute(total, "ctx", QUAD * d)
        others.append(other)
        d *= 2
        if d < n_groups:
            total = call(total_body, [("vmem", shape, F32)], [("vmem", total), ("vmem", other)], nbytes=1 << 19)[0]
    args = [("vmem", r) for r in received + others]
    if state is not None:
        args.append(("vmem", state))
    outs = call(
        functools.partial(spread_body, heads_own, forward, state is not None, len(others)),
        [("vmem", shape, F32)] * QUAD,
        args,
        nbytes=1 << 20,
    )
    return [outs[0]] + [xor_permute(outs[j], "ctx", j) for j in range(1, QUAD)]


def block(queries, keys, values, cotangent, state_in):
    tok, feat_here = queries.shape
    heads_here = feat_here // DH
    heads_own = heads_here // QUAD
    width = heads_own * DH
    n_head = lax.axis_size("head")
    feat_count = feat_here * n_head
    part = (heads_own, DH, DH)
    whole = ("vmem", (tok, feat_here), BF16)
    q, g = ("vmem", queries), ("vmem", cotangent)
    state_flops = 2 * tok * DH * DH * heads_own
    score_flops = 4 * tok * tok * DH * heads_own
    sums = ("vmem", part, F32)

    hbm = lambda x: pltpu.with_memory_space_constraint(x, pltpu.HBM)
    *kv_remote, k_here, v_here = call(
        functools.partial(outer_remote_body, heads_own),
        [sums] * (QUAD - 1) + [whole, whole],
        [("hbm", hbm(keys)), ("hbm", hbm(values))],
        flops=3 * state_flops,
        nbytes=3 * MIB,
        scratch=[pltpu.SemaphoreType.DMA((2, QUAD))],
    )
    k, v = ("vmem", k_here), ("vmem", v_here)
    kv_own = call(functools.partial(outer_own_body, heads_own), [sums], [k, v], flops=state_flops)[0]
    wide_f32 = ("vmem", (tok, width), F32)
    wide_low = ("vmem", (tok, width), BF16)
    state_low = ("vmem", part, BF16)
    rows = ("vmem", (tok, DH), F32)
    locals_, sts, qts = [], [], []
    for slot in FORWARD_PLACES:
        out, st, qt = call(
            functools.partial(local_attention_body, slot, heads_own),
            [wide_f32, ("vmem", (heads_own, tok, tok), BF16), ("vmem", (width, tok), BF16)],
            [q, k, v],
            flops=3 * score_flops // 2,
        )
        locals_.append(("vmem", out))
        sts.append(("vmem", st))
        qts.append(("vmem", qt))
    states = scan_quads(kv_remote, kv_own, heads_own, True, state_in)

    atts, lows = [], []
    acc = []
    for slot in range(QUAD):
        last = slot == QUAD - 1
        att, low, *acc = call(
            functools.partial(attend_body, slot, heads_own, slot == 0, last),
            [wide_f32, state_low] + ([("vmem", (2, tok), F32)] if last else [rows, rows]),
            [q, g, locals_[slot], ("vmem", states[slot])] + [("vmem", x) for x in acc],
            flops=state_flops,
        )
        atts.append(("vmem", att))
        lows.append(("vmem", low))
    stats = acc[0]
    all_stats = [stats] + [xor_permute(stats, "head", i) for i in range(1, n_head)]
    ds, qds = [None] * QUAD, [None] * QUAD
    norms = []
    for slots in NORM_PLACES:
        n = len(slots)
        first = not norms
        outs = call(
            functools.partial(norm_body, slots, heads_own, feat_count, n_head if first else 0),
            [wide_low] * n + [sums] * n + ([rows, rows] if first else []),
            [g]
            + [("vmem", x) for x in (all_stats if first else norms)]
            + [x[s] for x in (atts, qts) for s in slots],
            flops=n * state_flops,
        )
        for i, s in enumerate(slots):
            ds[s], qds[s] = outs[i], outs[n + i]
        if first:
            norms = outs[2 * n :]
    output = call(
        functools.partial(output_body, heads_own), [whole], [("vmem", norms[0])] + atts, nbytes=3 * MIB // 2
    )[0]
    gks, gvs = [None] * QUAD, [None] * QUAD
    grad_query = None
    for slot in BACKWARD_PLACES:
        args = [q, k, v, ("vmem", ds[slot]), lows[slot], sts[slot]]
        aliases = {}
        if grad_query is not None:
            aliases = {len(args): 0}
            args.append(("vmem", grad_query))
        grad_query, gk, gv = call(
            functools.partial(local_grads_body, slot, heads_own),
            [whole, wide_f32, wide_f32],
            args,
            flops=3 * score_flops,
            scratch=[VMEM((tok, tok), BF16)],
            aliases=aliases,
        )
        gks[slot], gvs[slot] = ("vmem", gk), ("vmem", gv)
    suffixes = scan_quads(qds[1:], qds[0], heads_own, False, None)
    full = ("hbm", (tok, feat_here), BF16)
    grads = ()
    for slot in range(QUAD):
        args = [k, v, gks[slot], gvs[slot], ("vmem", suffixes[slot])]
        aliases = {len(args) + i: i for i in range(len(grads))}
        args += [("hbm", x) for x in grads]
        grads = call(
            functools.partial(final_body, slot, heads_own),
            [full, full],
            args,
            flops=2 * state_flops,
            scratch=[
                VMEM((tok, width), BF16),
                VMEM((tok, width), BF16),
                pltpu.SemaphoreType.DMA((2, heads_own)),
            ],
            aliases=aliases,
        )
    return output, grad_query, grads[0], grads[1]


def solution(mesh):
    wide_spec = P("ctx", "head")
    return jax.shard_map(
        block,
        mesh=mesh,
        in_specs=(wide_spec,) * 4 + (P("head", None, None),),
        out_specs=(wide_spec,) * 4,
        check_vma=False,
    )
```
